256 devices in a mesh: ctx: 32 (over y, z), head: 8 (over x, core).
Axes of the slice: x: 4, y: 4, z: 8, core: 2. Of those that a mesh axis runs over, the one named last changes fastest.
Arguments:
- queries: bfloat16 [8192, 4096], P('ctx', 'head'), may hold values from -6 to 6
- key_rows: bfloat16 [8192, 4096], P('ctx', 'head'), may hold values from -0.5 to 0.5
- value_rows: bfloat16 [8192, 4096], P('ctx', 'head'), may hold values from -6 to 6
- doc_ids: int32 [8192], P('ctx'), may hold values from 0 to 15, never falling along the last dimension, each value on 1 to 2048 neighbouring positions
- out_grad: bfloat16 [8192, 6144], P(('ctx', 'head')), may hold values from -6 to 6
- out_weight: bfloat16 [4096, 6144], P('head', 'ctx'), may hold values from -0.09375 to 0.09375
Outputs:
- layer_out: bfloat16 [8192, 6144], P(('ctx', 'head'))
- query_grad: bfloat16 [8192, 4096], P('ctx', 'head')
- key_grad: bfloat16 [8192, 4096], P('ctx', 'head')
- value_grad: bfloat16 [8192, 4096], P('ctx', 'head')
- weight_grad: bfloat16 [4096, 6144], P(('head', 'ctx'))
The draws below stay inside these ranges and needn't reach their ends.
Inputs may be any that keep to these rules, and one draw needn't show every extreme that they name: `doc_ids`: repository ids never fall along the sequence; each repository covers 1 to 2048 tokens, and one covers exactly that many.
All inputs are finite; a program needn't handle non-finite values.
Results may differ from the reference program's by a relative error of at most 0.025.
Values may be sent and summed in bfloat16 or wider, within the bound.
No kernel may reach another device: no remote copies, remote signals or barrier semaphores. Data moves between devices by JAX's collectives and lax.ppermute only.
A program may use at most 128 MiB of HBM per device.

```python
import math
import jax
import jax.numpy as jnp
import numpy as np
from jax import lax

D = 6144
HEADS = 32
HD = 128
AW = 4096
TOK_DEV = 256
TOKENS = 8192
N_CTX = 32


def shard_levels(own_key, dims, cuts, least, high):
    factor_of, own = 1.0, jax.random.fold_in(own_key, 6)
    for axis_at, shards_of in cuts:
        heights = jnp.exp(jax.random.uniform(jax.random.fold_in(own, axis_at), (shards_of,), jnp.float32, least / len(cuts), high / len(cuts)))
        factor_of = factor_of * jnp.repeat(heights, dims[axis_at] // shards_of).reshape([-1 if axis == axis_at else 1 for axis in range(len(dims))])
    return factor_of


def length_profile(count, total, bound, slope):
    loads = [(1 << 20) // math.isqrt(rank ** slope) + 1 for rank in range(2, count + 1)]
    rest, counts = total - bound - (count - 1), [1] * (count - 1)
    while rest > 0:
        free = [i for i in range(count - 1) if counts[i] < bound]
        mass, budget = sum([loads[i] for i in free]), rest
        for i in free:
            more = min(bound - counts[i], max(1, budget * loads[i] // mass), rest)
            counts[i] = counts[i] + more
            rest = rest - more
    return np.array([bound] + counts)


def uneven_parts(rng, number_of, total, most, lean):
    if number_of == 2:
        one = jax.random.randint(rng, (), max(1, total - most), min(most, total - 1) + 1)
        return jnp.stack([one, total - one])
    tallies = jnp.asarray(length_profile(number_of, total, most, lean), jnp.int32)
    couples = (number_of - 1) // 2
    donor, sink = tallies[1:1 + 2 * couples:2], tallies[2:2 + 2 * couples:2]
    room = jnp.minimum(donor - 1, most - sink)
    shifted = jax.random.randint(jax.random.fold_in(rng, 1), (couples,), 0, 1 << 20) % (room + 1)
    tallies = tallies.at[1:1 + 2 * couples:2].set(donor - shifted).at[2:2 + 2 * couples:2].set(sink + shifted)
    return tallies[jax.random.permutation(jax.random.fold_in(rng, 2), number_of)]


def normal_values(stream_key, dims, scale, reach, cuts=(), kind=jnp.bfloat16):
    values = jax.random.normal(stream_key, dims, jnp.float32) * scale
    if len(cuts) > 0:
        values = shard_levels(stream_key, dims, cuts, -0.22, 0.18) * values
    return jnp.clip(values, min=-reach, max=reach).astype(kind)


def setup_inputs(seed: int = 0) -> dict:
    splits = jax.random.split(jax.random.key(seed), 7)
    queries = normal_values(splits[0], (TOKENS, AW), 1.0, 6.0, ((0, 32), (1, 8)))
    key_rows = normal_values(splits[1], (TOKENS, AW), HD ** -0.5, 0.5, ((0, 32), (1, 8)))
    value_rows = normal_values(splits[2], (TOKENS, AW), 1.0, 6.0, ((0, 32), (1, 8)))
    doc_ids = jnp.searchsorted(jnp.cumsum(uneven_parts(splits[3], N_CTX // 2, TOKENS, 8 * TOK_DEV, 2)), jnp.arange(TOKENS), side="right").astype(jnp.int32)
    out_grad = normal_values(splits[4], (TOKENS, D), 1.0, 6.0, ((0, 256),))
    out_weight = normal_values(splits[5], (AW, D), AW ** -0.5, 0.09375, ((0, 8), (1, 32)))
    return dict(queries=queries, key_rows=key_rows, value_rows=value_rows, doc_ids=doc_ids, out_grad=out_grad, out_weight=out_weight)


EPSILON = 1e-05

def block_allowed(block_docs):
    causal = jnp.tril(jnp.ones((TOK_DEV, TOK_DEV), dtype=bool))
    return causal & (block_docs[:, None] == block_docs[None, :])

def forward_head(query_head, key_head, value_head, doc_ids):
    query_blocks = query_head.reshape(N_CTX, TOK_DEV, HD)
    key_blocks = key_head.reshape(N_CTX, TOK_DEV, HD)
    value_blocks = value_head.reshape(N_CTX, TOK_DEV, HD)
    doc_blocks = doc_ids.reshape(N_CTX, TOK_DEV)

    def advance(carried, block_data):
        running_state, prior_last = carried
        query_block, key_block, value_block, block_docs = block_data
        allowed = block_allowed(block_docs)
        scores = jnp.dot(query_block, key_block.T, preferred_element_type=jnp.float32)
        weights = jnp.where(allowed, scores, 0.0).astype(jnp.bfloat16)
        entry_doc = block_docs[0]
        final_doc = block_docs[-1]
        prior_state = jnp.where(prior_last == entry_doc, running_state, jnp.float32(0.0)).astype(jnp.bfloat16)
        row_mask = (block_docs == prior_last)[:, None]
        inter = jnp.dot(query_block, prior_state, preferred_element_type=jnp.float32)
        mixed = jnp.dot(weights, value_block, preferred_element_type=jnp.float32) + jnp.where(row_mask, inter, jnp.float32(0.0))
        key_last = jnp.where((block_docs == final_doc)[:, None], key_block, jnp.zeros_like(key_block))
        local_state = jnp.dot(key_last.T, value_block, preferred_element_type=jnp.float32)
        new_state = local_state + jnp.where(prior_last == final_doc, running_state, jnp.float32(0.0))
        return ((new_state, final_doc), (mixed, prior_state))
    initial = (jnp.zeros((HD, HD), jnp.float32), jnp.array(-1, dtype=jnp.int32))
    carried, outputs = lax.scan(advance, initial, (query_blocks, key_blocks, value_blocks, doc_blocks))
    mixed, prior_states = outputs
    return (mixed.reshape(TOKENS, HD), prior_states)

def backward_head(query_head, key_head, value_head, grad_head, prior_states, doc_ids):
    query_blocks = query_head.reshape(N_CTX, TOK_DEV, HD)
    key_blocks = key_head.reshape(N_CTX, TOK_DEV, HD)
    value_blocks = value_head.reshape(N_CTX, TOK_DEV, HD)
    grad_blocks = grad_head.reshape(N_CTX, TOK_DEV, HD)
    doc_blocks = doc_ids.reshape(N_CTX, TOK_DEV)

    def advance(carried, block_data):
        future_state, later_first = carried
        query_block, key_block, value_block, grad_block, prior_block, block_docs = block_data
        allowed = block_allowed(block_docs)
        scores = jnp.dot(query_block, key_block.T, preferred_element_type=jnp.float32)
        weights = jnp.where(allowed, scores, 0.0).astype(jnp.bfloat16)
        grad_raw = jnp.dot(grad_block, value_block.T, preferred_element_type=jnp.float32)
        grad_scores = jnp.where(allowed, grad_raw, 0.0).astype(jnp.bfloat16)
        entry_doc = block_docs[0]
        final_doc = block_docs[-1]
        later_state = jnp.where(later_first == final_doc, future_state, jnp.float32(0.0)).astype(jnp.bfloat16)
        row_mask = (block_docs == entry_doc)[:, None]
        col_mask = (block_docs == later_first)[:, None]
        query_grad = jnp.dot(grad_scores, key_block, preferred_element_type=jnp.float32) + jnp.where(row_mask, jnp.dot(grad_block, prior_block.T, preferred_element_type=jnp.float32), jnp.float32(0.0))
        key_grad = jnp.dot(grad_scores.T, query_block, preferred_element_type=jnp.float32) + jnp.where(col_mask, jnp.dot(value_block, later_state.T, preferred_element_type=jnp.float32), jnp.float32(0.0))
        value_grad = jnp.dot(weights.T, grad_block, preferred_element_type=jnp.float32) + jnp.where(col_mask, jnp.dot(key_block, later_state, preferred_element_type=jnp.float32), jnp.float32(0.0))
        query_first = jnp.where(row_mask, query_block, jnp.zeros_like(query_block))
        local_state = jnp.dot(query_first.T, grad_block, preferred_element_type=jnp.float32)
        new_future = local_state + jnp.where(later_first == entry_doc, future_state, jnp.float32(0.0))
        return ((new_future, entry_doc), (query_grad.astype(jnp.bfloat16), key_grad.astype(jnp.bfloat16), value_grad.astype(jnp.bfloat16)))
    initial = (jnp.zeros((HD, HD), jnp.float32), jnp.array(-1, dtype=jnp.int32))
    carried, outputs = lax.scan(advance, initial, (query_blocks, key_blocks, value_blocks, grad_blocks, prior_states, doc_blocks), reverse=True)
    query_grad, key_grad, value_grad = outputs
    return (query_grad.reshape(TOKENS, HD), key_grad.reshape(TOKENS, HD), value_grad.reshape(TOKENS, HD))

def split_heads(matrix):
    return matrix.reshape(TOKENS, HEADS, HD).transpose(1, 0, 2)

def merge_heads(stacked):
    return stacked.transpose(1, 0, 2).reshape(TOKENS, AW)

def reference(queries, key_rows, value_rows, doc_ids, out_grad, out_weight):
    query_split = split_heads(queries)
    key_split = split_heads(key_rows)
    value_split = split_heads(value_rows)

    def forward_one(packed):
        return forward_head(packed[0], packed[1], packed[2], doc_ids)
    mixed, prior_states = lax.map(forward_one, (query_split, key_split, value_split))
    inv_norm = lax.rsqrt(lax.optimization_barrier(jnp.mean(mixed * mixed, axis=-1, keepdims=True)) + EPSILON)
    normed = mixed * inv_norm
    normed_flat = merge_heads(normed.astype(jnp.bfloat16))
    layer_out = jnp.dot(normed_flat, out_weight, preferred_element_type=jnp.float32).astype(jnp.bfloat16)
    grad_flat = jnp.dot(out_grad, out_weight.T, preferred_element_type=jnp.float32)
    grad_normed = split_heads(grad_flat)
    mixed_grad = (inv_norm * (grad_normed - normed * lax.optimization_barrier(jnp.mean(grad_normed * normed, axis=-1, keepdims=True)))).astype(jnp.bfloat16)

    def backward_one(packed):
        return backward_head(packed[0], packed[1], packed[2], packed[3], packed[4], doc_ids)
    query_grad, key_grad, value_grad = lax.map(backward_one, (query_split, key_split, value_split, mixed_grad, prior_states))

    def shard_term(running, packed):
        normed_block, grad_block = packed
        partial_sum = jnp.dot(normed_block.T, grad_block, preferred_element_type=jnp.float32).astype(jnp.bfloat16)
        partial_sum = lax.optimization_barrier(partial_sum)
        return (running + partial_sum.astype(jnp.float32), None)
    weight_sum, unused = lax.scan(shard_term, jnp.zeros((AW, D), jnp.float32), (normed_flat.reshape(N_CTX, TOK_DEV, AW), out_grad.reshape(N_CTX, TOK_DEV, D)))
    return (layer_out, merge_heads(query_grad), merge_heads(key_grad), merge_heads(value_grad), weight_sum.astype(jnp.bfloat16))
```

```python
import jax
import jax.numpy as jnp
from jax import lax
from jax.sharding import Mesh, PartitionSpec as P

HD = 128
EPSILON = 1e-05
BF = jnp.bfloat16
F32 = jnp.float32
WINDOW = (1, 2, 4)
CTX = ("y", "z")
HEAD = ("x", "c")


def shift(x, by):
    count = lax.axis_size(CTX)
    pairs = [(i, i + by) for i in range(count) if 0 <= i + by < count]
    return lax.ppermute(x, CTX, pairs)


def window_state(local, sent_mark, first_mark, enter_mark, direction):
    rows = local.shape[0]

    def packed(state, mark):
        return jnp.concatenate(
            [state.astype(BF), jnp.full((16, HD), 1.0, BF) * (mark + 1.0).astype(BF)], axis=0
        )

    def opened(message):
        return message[:rows].astype(F32), message[rows, 0].astype(F32) - 1.0

    state, mark = opened(shift(packed(local, sent_mark), direction))
    total = jnp.where(mark == enter_mark, state, 0.0)
    for step in WINDOW:
        state, mark = opened(shift(packed(total, first_mark), direction * step))
        total = total + jnp.where(mark == first_mark, state, 0.0)
    return total


def shards(queries, key_rows, value_rows, doc_ids, out_grad, out_weight):
    tok, width = queries.shape
    heads = width // HD
    ny, nz, nh = lax.axis_size("y"), lax.axis_size("z"), lax.axis_size(HEAD)
    cols = out_grad.shape[1] // ny
    sub = out_grad.shape[0]
    weight_t = lax.all_gather(out_weight.T, "z", axis=0, tiled=True)
    og = lax.all_to_all(out_grad.reshape(sub, ny, cols).transpose(1, 0, 2), "y", 0, 0)
    og = lax.all_gather(og.reshape(ny * sub, cols), HEAD, axis=0, tiled=True)

    query_heads = queries.reshape(tok, heads, HD)
    key_heads = key_rows.reshape(tok, heads, HD)
    value_heads = value_rows.reshape(tok, heads, HD)
    docs = doc_ids.astype(F32)
    first_doc, last_doc = docs[0], docs[-1]
    causal = jnp.tril(jnp.ones((tok, tok), dtype=bool))
    allowed = (causal & (doc_ids[:, None] == doc_ids[None, :]))[None]
    in_first = (docs == first_doc)[:, None, None]
    in_last = (docs == last_doc)[:, None, None]

    key_last = jnp.where(in_last, key_heads, jnp.zeros_like(key_heads))
    local_state = jnp.einsum("thd,the->hde", key_last, value_heads, preferred_element_type=F32)
    prior = window_state(
        local_state.reshape(heads * HD, HD), last_doc, first_doc, first_doc, 1
    ).astype(BF).reshape(heads, HD, HD)

    scores = jnp.einsum("thd,shd->hts", query_heads, key_heads, preferred_element_type=F32)
    weights = jnp.where(allowed, scores, F32(0.0)).astype(BF)
    inter = jnp.einsum("thd,hde->the", query_heads, prior, preferred_element_type=F32)
    mixed = jnp.einsum(
        "hts,she->the", weights, value_heads, preferred_element_type=F32
    ) + jnp.where(in_first, inter, F32(0.0))
    inv_norm = lax.rsqrt(jnp.mean(mixed * mixed, axis=-1, keepdims=True) + EPSILON)
    normed = mixed * inv_norm
    normed_flat = normed.astype(BF).reshape(tok, width)

    gn_part = jnp.dot(og, weight_t, preferred_element_type=F32).astype(BF)
    gn_part = gn_part.reshape(nh, ny, sub, width).transpose(1, 0, 2, 3)
    gn = lax.all_to_all(gn_part, "y", 0, 0)
    grad_normed = jnp.sum(gn.astype(F32), axis=0).reshape(tok, heads, HD)

    normed_all = lax.all_gather(normed_flat.reshape(nh, sub, width), "y", axis=1)
    normed_all = normed_all.reshape(nh * ny * sub, width)
    out_part = lax.dot_general(
        normed_all, weight_t, (((1,), (1,)), ((), ())), preferred_element_type=F32
    ).astype(BF)
    out_sum = lax.psum_scatter(out_part, HEAD, scatter_dimension=0, tiled=True)
    layer_out = lax.all_to_all(out_sum.reshape(ny, sub, cols), "y", 0, 0)
    layer_out = layer_out.transpose(1, 0, 2).reshape(sub, ny * cols)

    wg_part = lax.dot_general(
        normed_all, og, (((0,), (0,)), ((), ())), preferred_element_type=F32
    ).astype(BF)
    rows = width // (ny * nz)
    wg_part = wg_part.reshape(ny, nz, rows, cols).transpose(1, 0, 2, 3).reshape(width, cols)
    wg_sum = lax.psum_scatter(wg_part, "z", scatter_dimension=0, tiled=True)
    wg = lax.all_to_all(wg_sum.reshape(ny, rows, cols), "y", 0, 0)
    weight_grad = wg.transpose(1, 0, 2).reshape(rows, ny * cols)

    mixed_grad = (
        inv_norm * (grad_normed - normed * jnp.mean(grad_normed * normed, axis=-1, keepdims=True))
    ).astype(BF)
    query_first = jnp.where(in_first, query_heads, jnp.zeros_like(query_heads))
    local_future = jnp.einsum("thd,the->hde", query_first, mixed_grad, preferred_element_type=F32)
    future = window_state(
        local_future.reshape(heads * HD, HD), first_doc, last_doc, last_doc, -1
    ).astype(BF).reshape(heads, HD, HD)

    grad_raw = jnp.einsum("the,she->hts", mixed_grad, value_heads, preferred_element_type=F32)
    grad_scores = jnp.where(allowed, grad_raw, F32(0.0)).astype(BF)
    query_grad = jnp.einsum(
        "hts,shd->thd", grad_scores, key_heads, preferred_element_type=F32
    ) + jnp.where(
        in_first,
        jnp.einsum("the,hde->thd", mixed_grad, prior, preferred_element_type=F32),
        F32(0.0),
    )
    key_grad = jnp.einsum(
        "hts,thd->shd", grad_scores, query_heads, preferred_element_type=F32
    ) + jnp.where(
        in_last,
        jnp.einsum("she,hde->shd", value_heads, future, preferred_element_type=F32),
        F32(0.0),
    )
    value_grad = jnp.einsum(
        "hts,the->she", weights, mixed_grad, preferred_element_type=F32
    ) + jnp.where(
        in_last,
        jnp.einsum("shd,hde->she", key_heads, future, preferred_element_type=F32),
        F32(0.0),
    )
    return (
        layer_out,
        query_grad.astype(BF).reshape(tok, width),
        key_grad.astype(BF).reshape(tok, width),
        value_grad.astype(BF).reshape(tok, width),
        weight_grad,
    )


def solution(mesh):
    grid = Mesh(mesh.devices.reshape(4, 8, 4, 2), ("y", "z", "x", "c"))
    return jax.shard_map(
        shards,
        mesh=grid,
        in_specs=(
            P(CTX, HEAD),
            P(CTX, HEAD),
            P(CTX, HEAD),
            P(CTX),
            P(CTX + HEAD, None),
            P(HEAD, CTX),
        ),
        out_specs=(
            P(CTX + HEAD, None),
            P(CTX, HEAD),
            P(CTX, HEAD),
            P(CTX, HEAD),
            P(HEAD + CTX, None),
        ),
        check_vma=False,
    )
```

```python
import jax
import jax.numpy as jnp
from jax import lax
from jax.sharding import Mesh, PartitionSpec as P

HD = 128
EPSILON = 1e-05
BF = jnp.bfloat16
F32 = jnp.float32
CTX = ("y", "z")
HEAD = ("x", "c")
SWAP = [(0, 1), (1, 0)]


def turn(x, axis, by):
    count = lax.axis_size(axis)
    return lax.ppermute(x, axis, [(i, (i + by) % count) for i in range(count)])


def row_state(local, first_marks, last_marks, marks, backward, beside=()):
    nz, ny = lax.axis_size("z"), lax.axis_size("y")
    rows = local.shape[0] // nz
    slices = local.astype(BF).reshape(nz, rows, HD)
    if marks is not None:
        slices = jnp.concatenate(
            [slices, jnp.broadcast_to(marks[None], (nz,) + marks.shape)], axis=1
        )
    got = lax.all_to_all(slices, "z", 0, 0)
    if marks is not None:
        first_marks = got[:, rows, 0].astype(F32)
        last_marks = got[:, rows + 8, 0].astype(F32)
    states = got[:, :rows].astype(F32)
    place = jnp.arange(nz)
    if backward:
        takes = (first_marks[None, :] == last_marks[:, None]) & (place[None, :] > place[:, None])
        edge, enters, sends = first_marks[0], last_marks, first_marks
        pairs = [(i, i - 1) for i in range(1, ny)]
    else:
        takes = (last_marks[None, :] == first_marks[:, None]) & (place[None, :] < place[:, None])
        edge, enters, sends = last_marks[nz - 1], first_marks, last_marks
        pairs = [(i, i + 1) for i in range(ny - 1)]
    carry = jnp.sum(jnp.where((sends == edge)[:, None, None], states, 0.0), axis=0)
    message = jnp.concatenate([carry.astype(BF), jnp.zeros((16, HD), BF) + edge.astype(BF)])
    message = lax.ppermute(message, "y", pairs)
    inside = jnp.sum(jnp.where(takes[:, :, None, None], states[None], 0.0), axis=1)
    linked = (message[rows, 0].astype(F32) == enters)[:, None, None]
    total = inside + jnp.where(linked, message[None, :rows].astype(F32), 0.0)
    total, beside = lax.optimization_barrier((total.astype(BF), beside))
    out = lax.all_to_all(total, "z", 0, 0)
    return out.reshape(local.shape), first_marks, last_marks, beside


def shards(queries, key_rows, value_rows, doc_ids, out_grad, out_weight):
    tok, width = queries.shape
    heads = width // HD
    ny, nz, nx = lax.axis_size("y"), lax.axis_size("z"), lax.axis_size("x")
    cols = out_grad.shape[1] // ny
    sub = out_grad.shape[0]
    half = nx * ny * sub
    core = lax.axis_index("c")

    query_heads = queries.reshape(tok, heads, HD)
    key_heads = key_rows.reshape(tok, heads, HD)
    value_heads = value_rows.reshape(tok, heads, HD)
    docs = doc_ids.astype(F32)
    first_doc, last_doc = docs[0], docs[-1]
    causal = jnp.tril(jnp.ones((tok, tok), dtype=bool))
    allowed = (causal & (doc_ids[:, None] == doc_ids[None, :]))[None]
    in_first = (docs == first_doc)[:, None, None]
    in_last = (docs == last_doc)[:, None, None]

    weight_t = lax.all_gather(out_weight.T, "z", axis=0, tiled=True)
    pieces = out_grad.reshape(sub, ny, cols).transpose(1, 0, 2)
    row, place = lax.axis_index("y"), lax.axis_index("x")
    piece = [lax.dynamic_index_in_dim(pieces, row, 0, False)]
    for step in range(1, ny):
        sent = lax.dynamic_index_in_dim(pieces, (row - step) % ny, 0, False)
        piece.append(turn(sent, "y", -step))
    piece = jnp.stack(piece)

    key_last = jnp.where(in_last, key_heads, jnp.zeros_like(key_heads))
    local_state = jnp.einsum("thd,the->hde", key_last, value_heads, preferred_element_type=F32)
    ones = jnp.ones((8, HD), F32)
    marks = jnp.concatenate([ones * (first_doc + 1.0), ones * (last_doc + 1.0)]).astype(BF)
    og_own = [piece] + [turn(piece, "x", -step) for step in range(1, nx)]
    prior, first_marks, last_marks, og_own = row_state(
        local_state.reshape(heads * HD, HD), None, None, marks, False, og_own
    )
    og_own = jnp.stack(og_own).reshape(half, cols)
    og_other = lax.ppermute(og_own, "c", SWAP)
    prior = prior.reshape(heads, HD, HD)

    scores = jnp.einsum("thd,shd->hts", query_heads, key_heads, preferred_element_type=F32)
    weights = jnp.where(allowed, scores, F32(0.0)).astype(BF)
    inter = jnp.einsum("thd,hde->the", query_heads, prior, preferred_element_type=F32)
    mixed = jnp.einsum(
        "hts,she->the", weights, value_heads, preferred_element_type=F32
    ) + jnp.where(in_first, inter, F32(0.0))
    inv_norm = lax.rsqrt(jnp.mean(mixed * mixed, axis=-1, keepdims=True) + EPSILON)
    normed = mixed * inv_norm

    by_core = normed.astype(BF).reshape(nx, 2, sub, width).transpose(1, 0, 2, 3)
    by_core = jnp.where(core == 0, by_core, by_core[::-1])
    by_core = jnp.concatenate([by_core, by_core], axis=1)
    by_core = lax.dynamic_slice_in_dim(by_core, place, nx, 1)
    gn_part = jnp.stack(
        [jnp.dot(g, weight_t, preferred_element_type=F32).astype(BF) for g in (og_own, og_other)]
    )
    gn_part = gn_part.reshape(2, nx, ny, sub, width).transpose(2, 0, 1, 3, 4)
    normed_all = [by_core] + [turn(by_core, "y", -step) for step in range(1, ny)]
    normed_all = jnp.stack(normed_all, axis=2).reshape(2, half, width)
    gn_part, normed_all = lax.optimization_barrier((gn_part, normed_all))

    gn = gn_part[0].astype(F32)
    for step in range(1, ny):
        gn = gn + turn(gn_part[step], "y", step).astype(F32)
    gn = lax.dynamic_slice_in_dim(jnp.concatenate([gn, gn], axis=1), (nx - place) % nx, nx, 1)
    gn = jnp.where(core == 0, gn, gn[::-1])
    grad_normed = gn.transpose(1, 0, 2, 3).reshape(tok, heads, HD)

    def project(rows):
        return lax.dot_general(
            rows, weight_t, (((1,), (1,)), ((), ())), preferred_element_type=F32
        )

    wg_part = lax.dot_general(
        normed_all[0], og_own, (((0,), (0,)), ((), ())), preferred_element_type=F32
    ) + lax.dot_general(
        normed_all[1], og_other, (((0,), (0,)), ((), ())), preferred_element_type=F32
    )
    rows = width // (ny * nz)
    wg_part = wg_part.astype(BF).reshape(ny, nz, rows, cols).transpose(1, 0, 2, 3)
    wg_sum = lax.psum_scatter(wg_part.reshape(width, cols), "z", scatter_dimension=0, tiled=True)
    out_sent = lax.ppermute(project(normed_all[1]).astype(BF), "c", SWAP)
    out_own = (project(normed_all[0]) + out_sent.astype(F32)).astype(BF)
    out_own = out_own.reshape(nx, ny * sub, cols)
    out_sum = out_own[0].astype(F32)
    for step in range(1, nx):
        out_sum = out_sum + turn(out_own[step], "x", step).astype(F32)
    out_sum = out_sum.astype(BF).reshape(ny, sub, cols)
    out_sum = jnp.concatenate([out_sum, out_sum])
    out_sum = lax.dynamic_slice_in_dim(out_sum, (ny - row) % ny, ny, 0)
    last = jnp.concatenate(
        [out_sum, wg_sum.reshape(ny, rows, cols)], axis=1
    )
    last = lax.all_to_all(last, "y", 0, 0).transpose(1, 0, 2).reshape(sub + rows, ny * cols)
    layer_out, weight_grad = last[:sub], last[sub:]

    mixed_grad = (
        inv_norm * (grad_normed - normed * jnp.mean(grad_normed * normed, axis=-1, keepdims=True))
    ).astype(BF)
    query_first = jnp.where(in_first, query_heads, jnp.zeros_like(query_heads))
    local_future = jnp.einsum("thd,the->hde", query_first, mixed_grad, preferred_element_type=F32)
    future, unused, unused, unused = row_state(
        local_future.reshape(heads * HD, HD), first_marks, last_marks, None, True
    )
    future = future.reshape(heads, HD, HD)

    grad_raw = jnp.einsum("the,she->hts", mixed_grad, value_heads, preferred_element_type=F32)
    grad_scores = jnp.where(allowed, grad_raw, F32(0.0)).astype(BF)
    query_grad = jnp.einsum(
        "hts,shd->thd", grad_scores, key_heads, preferred_element_type=F32
    ) + jnp.where(
        in_first,
        jnp.einsum("the,hde->thd", mixed_grad, prior, preferred_element_type=F32),
        F32(0.0),
    )
    key_grad = jnp.einsum(
        "hts,thd->shd", grad_scores, query_heads, preferred_element_type=F32
    ) + jnp.where(
        in_last,
        jnp.einsum("she,hde->shd", value_heads, future, preferred_element_type=F32),
        F32(0.0),
    )
    value_grad = jnp.einsum(
        "hts,the->she", weights, mixed_grad, preferred_element_type=F32
    ) + jnp.where(
        in_last,
        jnp.einsum("shd,hde->she", key_heads, future, preferred_element_type=F32),
        F32(0.0),
    )
    return (
        layer_out,
        query_grad.astype(BF).reshape(tok, width),
        key_grad.astype(BF).reshape(tok, width),
        value_grad.astype(BF).reshape(tok, width),
        weight_grad,
    )


def solution(mesh):
    grid = Mesh(mesh.devices.reshape(4, 8, 4, 2), ("y", "z", "x", "c"))
    return jax.shard_map(
        shards,
        mesh=grid,
        in_specs=(
            P(CTX, HEAD),
            P(CTX, HEAD),
            P(CTX, HEAD),
            P(CTX),
            P(CTX + HEAD, None),
            P(HEAD, CTX),
        ),
        out_specs=(
            P(CTX + HEAD, None),
            P(CTX, HEAD),
            P(CTX, HEAD),
            P(CTX, HEAD),
            P(HEAD + CTX, None),
        ),
        check_vma=False,
    )
```

```python
import jax
import jax.numpy as jnp
from jax import lax
from jax.sharding import Mesh, PartitionSpec as P

HD = 128
EPSILON = 1e-05
BF = jnp.bfloat16
F32 = jnp.float32
CTX = ("y", "z")
HEAD = ("x", "c")
SWAP = [(0, 1), (1, 0)]


def turn(x, axis, by):
    count = lax.axis_size(axis)
    return lax.ppermute(x, axis, [(i, (i + by) % count) for i in range(count)])


def row_state(local, first_marks, last_marks, marks, backward, beside=()):
    nz, ny = lax.axis_size("z"), lax.axis_size("y")
    rows = local.shape[0] // nz
    slices = local.astype(BF).reshape(nz, rows, HD)
    if marks is not None:
        slices = jnp.concatenate(
            [slices, jnp.broadcast_to(marks[None], (nz,) + marks.shape)], axis=1
        )
    got = lax.all_to_all(slices, "z", 0, 0)
    if marks is not None:
        first_marks = got[:, rows, 0].astype(F32)
        last_marks = got[:, rows + 8, 0].astype(F32)
    states = got[:, :rows].astype(F32)
    place = jnp.arange(nz)
    if backward:
        takes = (first_marks[None, :] == last_marks[:, None]) & (place[None, :] > place[:, None])
        edge, enters, sends = first_marks[0], last_marks, first_marks
        pairs = [(i, i - 1) for i in range(1, ny)]
    else:
        takes = (last_marks[None, :] == first_marks[:, None]) & (place[None, :] < place[:, None])
        edge, enters, sends = last_marks[nz - 1], first_marks, last_marks
        pairs = [(i, i + 1) for i in range(ny - 1)]
    carry = jnp.sum(jnp.where((sends == edge)[:, None, None], states, 0.0), axis=0)
    message = jnp.concatenate([carry.astype(BF), jnp.zeros((16, HD), BF) + edge.astype(BF)])
    message = lax.ppermute(message, "y", pairs)
    inside = jnp.sum(jnp.where(takes[:, :, None, None], states[None], 0.0), axis=1)
    linked = (message[rows, 0].astype(F32) == enters)[:, None, None]
    total = inside + jnp.where(linked, message[None, :rows].astype(F32), 0.0)
    total, beside = lax.optimization_barrier((total.astype(BF), beside))
    out = lax.all_to_all(total, "z", 0, 0)
    return out.reshape(local.shape), first_marks, last_marks, beside


def shards(queries, key_rows, value_rows, doc_ids, out_grad, out_weight):
    tok, width = queries.shape
    heads = width // HD
    ny, nz, nx = lax.axis_size("y"), lax.axis_size("z"), lax.axis_size("x")
    cols = out_grad.shape[1] // ny
    sub = out_grad.shape[0]
    half = nx * ny * sub
    core = lax.axis_index("c")

    weight_here, key_rows = lax.optimization_barrier((out_weight.T, key_rows))
    weight_t = lax.all_gather(weight_here, "z", axis=0, tiled=True)
    query_heads = queries.reshape(tok, heads, HD)
    key_heads = key_rows.reshape(tok, heads, HD)
    value_heads = value_rows.reshape(tok, heads, HD)
    docs = doc_ids.astype(F32)
    first_doc, last_doc = docs[0], docs[-1]
    causal = jnp.tril(jnp.ones((tok, tok), dtype=bool))
    allowed = (causal & (doc_ids[:, None] == doc_ids[None, :]))[None]
    in_first = (docs == first_doc)[:, None, None]
    in_last = (docs == last_doc)[:, None, None]

    pieces = out_grad.reshape(sub, ny, cols).transpose(1, 0, 2)
    key_last = jnp.where(in_last, key_heads, jnp.zeros_like(key_heads))
    local_state = jnp.einsum("thd,the->hde", key_last, value_heads, preferred_element_type=F32)
    pieces, local_state = lax.optimization_barrier((pieces, local_state.astype(BF)))
    row, place = lax.axis_index("y"), lax.axis_index("x")
    piece = [lax.dynamic_index_in_dim(pieces, row, 0, False)]
    for step in range(1, ny):
        sent = lax.dynamic_index_in_dim(pieces, (row - step) % ny, 0, False)
        piece.append(turn(sent, "y", -step))
    piece = jnp.stack(piece + piece)
    piece = lax.dynamic_slice_in_dim(piece, (ny - row) % ny, ny, 0)
    ones = jnp.ones((8, HD), F32)
    marks = jnp.concatenate([ones * (first_doc + 1.0), ones * (last_doc + 1.0)]).astype(BF)
    og_own = [piece] + [turn(piece, "x", -step) for step in range(1, nx)]
    prior, first_marks, last_marks, (og_own, weight_t) = row_state(
        local_state.reshape(heads * HD, HD), None, None, marks, False, (og_own, weight_t)
    )
    og_own = jnp.stack(og_own).reshape(half, cols)
    og_other = lax.ppermute(og_own, "c", SWAP)
    gn_part = jnp.stack(
        [jnp.dot(g, weight_t, preferred_element_type=F32).astype(BF) for g in (og_own, og_other)]
    )
    gn_part = gn_part.reshape(2, nx, ny, sub, width).transpose(2, 0, 1, 3, 4)
    prior = prior.reshape(heads, HD, HD)

    scores = jnp.einsum("thd,shd->hts", query_heads, key_heads, preferred_element_type=F32)
    weights = jnp.where(allowed, scores, F32(0.0)).astype(BF)
    inter = jnp.einsum("thd,hde->the", query_heads, prior, preferred_element_type=F32)
    mixed = jnp.einsum(
        "hts,she->the", weights, value_heads, preferred_element_type=F32
    ) + jnp.where(in_first, inter, F32(0.0))
    inv_norm = lax.rsqrt(jnp.mean(mixed * mixed, axis=-1, keepdims=True) + EPSILON)
    normed = mixed * inv_norm

    by_core = normed.astype(BF).reshape(nx, 2, sub, width).transpose(1, 0, 2, 3)
    by_core = jnp.where(core == 0, by_core, by_core[::-1])
    by_core = jnp.concatenate([by_core, by_core], axis=1)
    by_core = lax.dynamic_slice_in_dim(by_core, place, nx, 1)
    by_core = jnp.broadcast_to(by_core[None], (ny,) + by_core.shape)
    normed_all = lax.all_to_all(by_core, "y", 0, 0).transpose(1, 2, 0, 3, 4)
    normed_all = normed_all.reshape(2, half, width)
    gn = lax.psum_scatter(
        gn_part.reshape(ny * tok, width), "y", scatter_dimension=0, tiled=True
    )
    gn, normed_all = lax.optimization_barrier((gn, normed_all))

    def project(rows):
        return lax.dot_general(
            rows, weight_t, (((1,), (1,)), ((), ())), preferred_element_type=F32
        )

    wg_part = lax.dot_general(
        normed_all[0], og_own, (((0,), (0,)), ((), ())), preferred_element_type=F32
    ) + lax.dot_general(
        normed_all[1], og_other, (((0,), (0,)), ((), ())), preferred_element_type=F32
    )
    rows = width // (ny * nz)
    wg_part = wg_part.astype(BF).reshape(ny, nz, rows, cols).transpose(1, 0, 2, 3)
    gn, normed_all, wg_part = lax.optimization_barrier(
        (gn, normed_all, wg_part.reshape(width, cols))
    )
    gn = gn.astype(F32).reshape(2, nx, sub, width)
    gn = lax.dynamic_slice_in_dim(jnp.concatenate([gn, gn], axis=1), (nx - place) % nx, nx, 1)
    gn = jnp.where(core == 0, gn, gn[::-1])
    grad_normed = gn.transpose(1, 0, 2, 3).reshape(tok, heads, HD)

    mixed_grad = (
        inv_norm * (grad_normed - normed * jnp.mean(grad_normed * normed, axis=-1, keepdims=True))
    ).astype(BF)
    query_first = jnp.where(in_first, query_heads, jnp.zeros_like(query_heads))
    local_future = jnp.einsum("thd,the->hde", query_first, mixed_grad, preferred_element_type=F32)
    wg_sum = lax.psum_scatter(wg_part, "z", scatter_dimension=0, tiled=True)
    out_sent = lax.ppermute(project(normed_all[1]).astype(BF), "c", SWAP)
    out_sent, local_future = lax.optimization_barrier((out_sent, local_future.astype(BF)))
    out_own = (project(normed_all[0]) + out_sent.astype(F32)).astype(BF)
    out_own = out_own.reshape(nx, ny * sub, cols)
    out_sum = out_own[0].astype(F32)
    for step in range(1, nx):
        out_sum = out_sum + turn(out_own[step], "x", step).astype(F32)
    out_sum = out_sum.astype(BF).reshape(ny, sub, cols)
    future, unused, unused, unused = row_state(
        local_future.reshape(heads * HD, HD), first_marks, last_marks, None, True
    )
    last = jnp.concatenate(
        [out_sum, wg_sum.reshape(ny, rows, cols)], axis=1
    )
    blocks = [None] * ny
    for step in range(ny):
        block = lax.dynamic_index_in_dim(last, (row + step) % ny, 0, False)
        blocks[-step] = turn(block, "y", step) if step else block
    last = lax.dynamic_slice_in_dim(jnp.stack(blocks + blocks), (ny - row) % ny, ny, 0)
    last = last.transpose(1, 0, 2).reshape(sub + rows, ny * cols)
    layer_out, weight_grad = last[:sub], last[sub:]

    future = future.reshape(heads, HD, HD)

    grad_raw = jnp.einsum("the,she->hts", mixed_grad, value_heads, preferred_element_type=F32)
    grad_scores = jnp.where(allowed, grad_raw, F32(0.0)).astype(BF)
    query_grad = jnp.einsum(
        "hts,shd->thd", grad_scores, key_heads, preferred_element_type=F32
    ) + jnp.where(
        in_first,
        jnp.einsum("the,hde->thd", mixed_grad, prior, preferred_element_type=F32),
        F32(0.0),
    )
    key_grad = jnp.einsum(
        "hts,thd->shd", grad_scores, query_heads, preferred_element_type=F32
    ) + jnp.where(
        in_last,
        jnp.einsum("she,hde->shd", value_heads, future, preferred_element_type=F32),
        F32(0.0),
    )
    value_grad = jnp.einsum(
        "hts,the->she", weights, mixed_grad, preferred_element_type=F32
    ) + jnp.where(
        in_last,
        jnp.einsum("shd,hde->she", key_heads, future, preferred_element_type=F32),
        F32(0.0),
    )
    return (
        layer_out,
        query_grad.astype(BF).reshape(tok, width),
        key_grad.astype(BF).reshape(tok, width),
        value_grad.astype(BF).reshape(tok, width),
        weight_grad,
    )


def solution(mesh):
    grid = Mesh(mesh.devices.reshape(4, 8, 4, 2), ("y", "z", "x", "c"))
    return jax.shard_map(
        shards,
        mesh=grid,
        in_specs=(
            P(CTX, HEAD),
            P(CTX, HEAD),
            P(CTX, HEAD),
            P(CTX),
            P(CTX + HEAD, None),
            P(HEAD, CTX),
        ),
        out_specs=(
            P(CTX + HEAD, None),
            P(CTX, HEAD),
            P(CTX, HEAD),
            P(CTX, HEAD),
            P(HEAD + CTX, None),
        ),
        check_vma=False,
    )
```

```python
import jax
import jax.numpy as jnp
from jax import lax
from jax.sharding import Mesh, PartitionSpec as P

HD = 128
EPSILON = 1e-05
BF = jnp.bfloat16
F32 = jnp.float32
CTX = ("y", "z")
HEAD = ("x", "c")
SWAP = [(0, 1), (1, 0)]


def turn(x, axis, by):
    count = lax.axis_size(axis)
    return lax.ppermute(x, axis, [(i, (i + by) % count) for i in range(count)])


def row_state(local, first_marks, last_marks, marks, backward, beside=()):
    nz, ny = lax.axis_size("z"), lax.axis_size("y")
    rows = local.shape[0] // nz
    slices = local.astype(BF).reshape(nz, rows, HD)
    if marks is not None:
        slices = jnp.concatenate(
            [slices, jnp.broadcast_to(marks[None], (nz,) + marks.shape)], axis=1
        )
    got = lax.all_to_all(slices, "z", 0, 0)
    if marks is not None:
        first_marks = got[:, rows, 0].astype(F32)
        last_marks = got[:, rows + 8, 0].astype(F32)
    states = got[:, :rows].astype(F32)
    place = jnp.arange(nz)
    if backward:
        takes = (first_marks[None, :] == last_marks[:, None]) & (place[None, :] > place[:, None])
        edge, enters, sends = first_marks[0], last_marks, first_marks
        pairs = [(i, i - 1) for i in range(1, ny)]
    else:
        takes = (last_marks[None, :] == first_marks[:, None]) & (place[None, :] < place[:, None])
        edge, enters, sends = last_marks[nz - 1], first_marks, last_marks
        pairs = [(i, i + 1) for i in range(ny - 1)]
    carry = jnp.sum(jnp.where((sends == edge)[:, None, None], states, 0.0), axis=0)
    message = jnp.concatenate([carry.astype(BF), jnp.zeros((16, HD), BF) + edge.astype(BF)])
    message = lax.ppermute(message, "y", pairs)
    inside = jnp.sum(jnp.where(takes[:, :, None, None], states[None], 0.0), axis=1)
    linked = (message[rows, 0].astype(F32) == enters)[:, None, None]
    total = inside + jnp.where(linked, message[None, :rows].astype(F32), 0.0)
    total, beside = lax.optimization_barrier((total.astype(BF), beside))
    out = lax.all_to_all(total, "z", 0, 0)
    return out.reshape(local.shape), first_marks, last_marks, beside


def shards(queries, key_rows, value_rows, doc_ids, out_grad, out_weight):
    tok, width = queries.shape
    heads = width // HD
    ny, nz, nx = lax.axis_size("y"), lax.axis_size("z"), lax.axis_size("x")
    cols = out_grad.shape[1] // ny
    sub = out_grad.shape[0]
    half = nx * ny * sub
    core = lax.axis_index("c")

    weight_here, key_rows = lax.optimization_barrier((out_weight.T, key_rows))
    weight_t = lax.all_gather(weight_here, "z", axis=0, tiled=True)
    query_heads = queries.reshape(tok, heads, HD)
    key_heads = key_rows.reshape(tok, heads, HD)
    value_heads = value_rows.reshape(tok, heads, HD)
    docs = doc_ids.astype(F32)
    first_doc, last_doc = docs[0], docs[-1]
    causal = jnp.tril(jnp.ones((tok, tok), dtype=bool))
    in_first = (docs == first_doc)[:, None, None]
    in_last = (docs == last_doc)[:, None, None]

    pieces = out_grad.reshape(sub, ny, cols).transpose(1, 0, 2)
    key_last = jnp.where(in_last, key_heads, jnp.zeros_like(key_heads))
    local_state = jnp.einsum("thd,the->hde", key_last, value_heads, preferred_element_type=F32)
    pieces, local_state, block_docs = lax.optimization_barrier(
        (pieces, local_state.astype(BF), doc_ids)
    )
    allowed = (causal & (block_docs[:, None] == block_docs[None, :]))[None]
    row, place = lax.axis_index("y"), lax.axis_index("x")
    piece = [lax.dynamic_index_in_dim(pieces, row, 0, False)]
    for step in range(1, ny):
        sent = lax.dynamic_index_in_dim(pieces, (row - step) % ny, 0, False)
        piece.append(turn(sent, "y", -step))
    piece = jnp.stack(piece + piece)
    piece = lax.dynamic_slice_in_dim(piece, (ny - row) % ny, ny, 0)
    ones = jnp.ones((8, HD), F32)
    marks = jnp.concatenate([ones * (first_doc + 1.0), ones * (last_doc + 1.0)]).astype(BF)
    og_own = [piece] + [turn(piece, "x", -step) for step in range(1, nx)]
    prior, first_marks, last_marks, (og_own, weight_t) = row_state(
        local_state.reshape(heads * HD, HD), None, None, marks, False, (og_own, weight_t)
    )
    og_own = jnp.stack(og_own).reshape(half, cols)
    og_other = lax.ppermute(og_own, "c", SWAP)
    gn_part = jnp.stack(
        [jnp.dot(g, weight_t, preferred_element_type=F32).astype(BF) for g in (og_own, og_other)]
    )
    gn_part = gn_part.reshape(2, nx, ny, sub, width).transpose(2, 0, 1, 3, 4)
    prior = prior.reshape(heads, HD, HD)

    scores = jnp.einsum("thd,shd->hts", query_heads, key_heads, preferred_element_type=F32)
    weights = jnp.where(allowed, scores, F32(0.0)).astype(BF)
    inter = jnp.einsum("thd,hde->the", query_heads, prior, preferred_element_type=F32)
    mixed = jnp.einsum(
        "hts,she->the", weights, value_heads, preferred_element_type=F32
    ) + jnp.where(in_first, inter, F32(0.0))
    inv_norm = lax.rsqrt(jnp.mean(mixed * mixed, axis=-1, keepdims=True) + EPSILON)
    normed = mixed * inv_norm

    by_core = normed.astype(BF).reshape(nx, 2, sub, width).transpose(1, 0, 2, 3)
    by_core = jnp.where(core == 0, by_core, by_core[::-1])
    by_core = jnp.concatenate([by_core, by_core], axis=1)
    by_core = lax.dynamic_slice_in_dim(by_core, place, nx, 1)
    by_core = jnp.broadcast_to(by_core[None], (ny,) + by_core.shape)
    normed_all = lax.all_to_all(by_core, "y", 0, 0).transpose(1, 2, 0, 3, 4)
    normed_all = normed_all.reshape(2, half, width)
    gn = lax.psum_scatter(
        gn_part.reshape(ny * tok, width), "y", scatter_dimension=0, tiled=True
    )
    gn, normed_all = lax.optimization_barrier((gn, normed_all))

    def project(rows):
        return lax.dot_general(
            rows, weight_t, (((1,), (1,)), ((), ())), preferred_element_type=F32
        )

    wg_part = lax.dot_general(
        normed_all[0], og_own, (((0,), (0,)), ((), ())), preferred_element_type=F32
    ) + lax.dot_general(
        normed_all[1], og_other, (((0,), (0,)), ((), ())), preferred_element_type=F32
    )
    rows = width // (ny * nz)
    wg_part = wg_part.astype(BF).reshape(ny, nz, rows, cols).transpose(1, 0, 2, 3)
    gn, normed_all, wg_part = lax.optimization_barrier(
        (gn, normed_all, wg_part.reshape(width, cols))
    )
    gn = gn.astype(F32).reshape(2, nx, sub, width)
    gn = lax.dynamic_slice_in_dim(jnp.concatenate([gn, gn], axis=1), (nx - place) % nx, nx, 1)
    gn = jnp.where(core == 0, gn, gn[::-1])
    grad_normed = gn.transpose(1, 0, 2, 3).reshape(tok, heads, HD)

    mixed_grad = (
        inv_norm * (grad_normed - normed * jnp.mean(grad_normed * normed, axis=-1, keepdims=True))
    ).astype(BF)
    query_first = jnp.where(in_first, query_heads, jnp.zeros_like(query_heads))
    local_future = jnp.einsum("thd,the->hde", query_first, mixed_grad, preferred_element_type=F32)
    wg_sum = lax.psum_scatter(wg_part, "z", scatter_dimension=0, tiled=True)
    out_sent = lax.ppermute(project(normed_all[1]).astype(BF), "c", SWAP)
    out_sent, local_future = lax.optimization_barrier((out_sent, local_future.astype(BF)))
    out_own = (project(normed_all[0]) + out_sent.astype(F32)).astype(BF)
    out_own = out_own.reshape(nx, ny * sub, cols)
    out_sum = out_own[0].astype(F32)
    for step in range(1, nx):
        out_sum = out_sum + turn(out_own[step], "x", step).astype(F32)
    out_sum = out_sum.astype(BF).reshape(ny, sub, cols)
    future, unused, unused, unused = row_state(
        local_future.reshape(heads * HD, HD), first_marks, last_marks, None, True
    )
    last = jnp.concatenate(
        [out_sum, wg_sum.reshape(ny, rows, cols)], axis=1
    )
    future, last = lax.optimization_barrier((future, last))
    blocks = [None] * ny
    for step in range(ny):
        block = lax.dynamic_index_in_dim(last, (row + step) % ny, 0, False)
        blocks[-step] = turn(block, "y", step) if step else block
    last = lax.dynamic_slice_in_dim(jnp.stack(blocks + blocks), (ny - row) % ny, ny, 0)
    last = last.transpose(1, 0, 2).reshape(sub + rows, ny * cols)
    layer_out, weight_grad = last[:sub], last[sub:]

    future = future.reshape(heads, HD, HD)

    grad_raw = jnp.einsum("the,she->hts", mixed_grad, value_heads, preferred_element_type=F32)
    grad_scores = jnp.where(allowed, grad_raw, F32(0.0)).astype(BF)
    query_grad = jnp.einsum(
        "hts,shd->thd", grad_scores, key_heads, preferred_element_type=F32
    ) + jnp.where(
        in_first,
        jnp.einsum("the,hde->thd", mixed_grad, prior, preferred_element_type=F32),
        F32(0.0),
    )
    key_grad = jnp.einsum(
        "hts,thd->shd", grad_scores, query_heads, preferred_element_type=F32
    ) + jnp.where(
        in_last,
        jnp.einsum("she,hde->shd", value_heads, future, preferred_element_type=F32),
        F32(0.0),
    )
    value_grad = jnp.einsum(
        "hts,the->she", weights, mixed_grad, preferred_element_type=F32
    ) + jnp.where(
        in_last,
        jnp.einsum("shd,hde->she", key_heads, future, preferred_element_type=F32),
        F32(0.0),
    )
    return (
        layer_out,
        query_grad.astype(BF).reshape(tok, width),
        key_grad.astype(BF).reshape(tok, width),
        value_grad.astype(BF).reshape(tok, width),
        weight_grad,
    )


def solution(mesh):
    grid = Mesh(mesh.devices.reshape(4, 8, 4, 2), ("y", "z", "x", "c"))
    return jax.shard_map(
        shards,
        mesh=grid,
        in_specs=(
            P(CTX, HEAD),
            P(CTX, HEAD),
            P(CTX, HEAD),
            P(CTX),
            P(CTX + HEAD, None),
            P(HEAD, CTX),
        ),
        out_specs=(
            P(CTX + HEAD, None),
            P(CTX, HEAD),
            P(CTX, HEAD),
            P(CTX, HEAD),
            P(HEAD + CTX, None),
        ),
        check_vma=False,
    )
```

```python
import jax
import jax.numpy as jnp
from jax import lax
from jax.sharding import Mesh, PartitionSpec as P

HD = 128
EPSILON = 1e-05
BF = jnp.bfloat16
F32 = jnp.float32
CTX = ("y", "z")
HEAD = ("x", "c")
SWAP = [(0, 1), (1, 0)]


def turn(x, axis, by):
    count = lax.axis_size(axis)
    return lax.ppermute(x, axis, [(i, (i + by) % count) for i in range(count)])


def row_state(local, first_marks, last_marks, marks, backward, beside=()):
    nz, ny = lax.axis_size("z"), lax.axis_size("y")
    rows = local.shape[0] // nz
    slices = local.astype(BF).reshape(nz, rows, HD)
    if marks is not None:
        slices = jnp.concatenate(
            [slices, jnp.broadcast_to(marks[None], (nz,) + marks.shape)], axis=1
        )
    got = lax.all_to_all(slices, "z", 0, 0)
    if marks is not None:
        first_marks = got[:, rows, 0].astype(F32)
        last_marks = got[:, rows + 8, 0].astype(F32)
    states = got[:, :rows].astype(F32)
    place = jnp.arange(nz)
    if backward:
        takes = (first_marks[None, :] == last_marks[:, None]) & (place[None, :] > place[:, None])
        edge, enters, sends = first_marks[0], last_marks, first_marks
        pairs = [(i, i - 1) for i in range(1, ny)]
    else:
        takes = (last_marks[None, :] == first_marks[:, None]) & (place[None, :] < place[:, None])
        edge, enters, sends = last_marks[nz - 1], first_marks, last_marks
        pairs = [(i, i + 1) for i in range(ny - 1)]
    carry = jnp.sum(jnp.where((sends == edge)[:, None, None], states, 0.0), axis=0)
    message = jnp.concatenate([carry.astype(BF), jnp.zeros((16, HD), BF) + edge.astype(BF)])
    message = lax.ppermute(message, "y", pairs)
    inside = jnp.sum(jnp.where(takes[:, :, None, None], states[None], 0.0), axis=1)
    linked = (message[rows, 0].astype(F32) == enters)[:, None, None]
    total = inside + jnp.where(linked, message[None, :rows].astype(F32), 0.0)
    total, beside = lax.optimization_barrier((total.astype(BF), beside))
    out = lax.all_to_all(total, "z", 0, 0)
    return out.reshape(local.shape), first_marks, last_marks, beside


def shards(queries, key_rows, value_rows, doc_ids, out_grad, out_weight):
    tok, width = queries.shape
    heads = width // HD
    ny, nz, nx = lax.axis_size("y"), lax.axis_size("z"), lax.axis_size("x")
    cols = out_grad.shape[1] // ny
    sub = out_grad.shape[0]
    half = nx * ny * sub
    core = lax.axis_index("c")

    weight_here, key_rows = lax.optimization_barrier((out_weight.T, key_rows))
    weight_t = lax.all_gather(weight_here, "z", axis=0, tiled=True)
    query_heads = queries.reshape(tok, heads, HD)
    key_heads = key_rows.reshape(tok, heads, HD)
    value_heads = value_rows.reshape(tok, heads, HD)
    docs = doc_ids.astype(F32)
    first_doc, last_doc = docs[0], docs[-1]
    causal = jnp.tril(jnp.ones((tok, tok), dtype=bool))
    in_first = (docs == first_doc)[:, None, None]
    in_last = (docs == last_doc)[:, None, None]

    pieces = out_grad.reshape(sub, ny, cols).transpose(1, 0, 2)
    key_last = jnp.where(in_last, key_heads, jnp.zeros_like(key_heads))
    local_state = jnp.einsum("thd,the->hde", key_last, value_heads, preferred_element_type=F32)
    pieces, local_state, block_docs = lax.optimization_barrier(
        (pieces, local_state.astype(BF), doc_ids)
    )
    allowed = (causal & (block_docs[:, None] == block_docs[None, :]))[None]
    row, place = lax.axis_index("y"), lax.axis_index("x")
    piece = [lax.dynamic_index_in_dim(pieces, row, 0, False)]
    for step in range(1, ny):
        sent = lax.dynamic_index_in_dim(pieces, (row - step) % ny, 0, False)
        piece.append(turn(sent, "y", -step))
    piece = jnp.stack(piece + piece)
    piece = lax.dynamic_slice_in_dim(piece, (ny - row) % ny, ny, 0)
    ones = jnp.ones((8, HD), F32)
    marks = jnp.concatenate([ones * (first_doc + 1.0), ones * (last_doc + 1.0)]).astype(BF)
    og_own = [piece] + [turn(piece, "x", -step) for step in range(1, nx)]
    prior, first_marks, last_marks, (og_own, weight_t) = row_state(
        local_state.reshape(heads * HD, HD), None, None, marks, False, (og_own, weight_t)
    )
    og_own = jnp.stack(og_own).reshape(half, cols)
    og_other = lax.ppermute(og_own, "c", SWAP)
    gn_part = jnp.stack(
        [jnp.dot(g, weight_t, preferred_element_type=F32).astype(BF) for g in (og_own, og_other)]
    )
    gn_part = gn_part.reshape(2, nx, ny, sub, width).transpose(2, 0, 1, 3, 4)
    prior = prior.reshape(heads, HD, HD)

    scores = jnp.einsum("thd,shd->hts", query_heads, key_heads, preferred_element_type=F32)
    weights = jnp.where(allowed, scores, F32(0.0)).astype(BF)
    inter = jnp.einsum("thd,hde->the", query_heads, prior, preferred_element_type=F32)
    mixed = jnp.einsum(
        "hts,she->the", weights, value_heads, preferred_element_type=F32
    ) + jnp.where(in_first, inter, F32(0.0))
    inv_norm = lax.rsqrt(jnp.mean(mixed * mixed, axis=-1, keepdims=True) + EPSILON)
    normed = mixed * inv_norm

    by_core = normed.astype(BF).reshape(nx, 2, sub, width).transpose(1, 0, 2, 3)
    by_core = jnp.where(core == 0, by_core, by_core[::-1])
    by_core = jnp.concatenate([by_core, by_core], axis=1)
    by_core = lax.dynamic_slice_in_dim(by_core, place, nx, 1)
    by_core = jnp.broadcast_to(by_core[None], (ny,) + by_core.shape)
    normed_all = lax.all_to_all(by_core, "y", 0, 0).transpose(1, 2, 0, 3, 4)
    normed_all = normed_all.reshape(2, half, width)
    gn = lax.psum_scatter(
        gn_part.reshape(ny * tok, width), "y", scatter_dimension=0, tiled=True
    )
    gn, normed_all = lax.optimization_barrier((gn, normed_all))

    def project(rows):
        return lax.dot_general(
            rows, weight_t, (((1,), (1,)), ((), ())), preferred_element_type=F32
        )

    wg_part = lax.dot_general(
        normed_all[0], og_own, (((0,), (0,)), ((), ())), preferred_element_type=F32
    ) + lax.dot_general(
        normed_all[1], og_other, (((0,), (0,)), ((), ())), preferred_element_type=F32
    )
    rows = width // (ny * nz)
    wg_part = wg_part.astype(BF).reshape(ny, nz, rows, cols).transpose(1, 0, 2, 3)
    gn, normed_all, wg_part = lax.optimization_barrier(
        (gn, normed_all, wg_part.reshape(width, cols))
    )
    gn = gn.astype(F32).reshape(2, nx, sub, width)
    gn = lax.dynamic_slice_in_dim(jnp.concatenate([gn, gn], axis=1), (nx - place) % nx, nx, 1)
    gn = jnp.where(core == 0, gn, gn[::-1])
    grad_normed = gn.transpose(1, 0, 2, 3).reshape(tok, heads, HD)

    mixed_grad = (
        inv_norm * (grad_normed - normed * jnp.mean(grad_normed * normed, axis=-1, keepdims=True))
    ).astype(BF)
    query_first = jnp.where(in_first, query_heads, jnp.zeros_like(query_heads))
    local_future = jnp.einsum("thd,the->hde", query_first, mixed_grad, preferred_element_type=F32)
    wg_sum = lax.psum_scatter(wg_part, "z", scatter_dimension=0, tiled=True)
    out_sent = lax.ppermute(project(normed_all[1]).astype(BF), "c", SWAP)
    out_sent, local_future = lax.optimization_barrier((out_sent, local_future.astype(BF)))
    out_own = (project(normed_all[0]) + out_sent.astype(F32)).astype(BF)
    out_own = out_own.reshape(nx, ny * sub, cols)
    out_sum = out_own[0].astype(F32)
    for step in range(1, nx):
        out_sum = out_sum + turn(out_own[step], "x", step).astype(F32)
    out_sum = out_sum.astype(BF).reshape(ny, sub, cols)
    future, unused, unused, unused = row_state(
        local_future.reshape(heads * HD, HD), first_marks, last_marks, None, True
    )
    last = jnp.concatenate(
        [out_sum, wg_sum.reshape(ny, rows, cols)], axis=1
    )
    future, last = lax.optimization_barrier((future, last))
    blocks = [None] * ny
    for step in range(ny):
        block = lax.dynamic_index_in_dim(last, (row + step) % ny, 0, False)
        blocks[-step] = turn(block, "y", step) if step else block
    last = [lax.select_n((slot - row) % ny, *blocks) for slot in range(ny)]
    last = jnp.concatenate(last, axis=1)
    layer_out, weight_grad = last[:sub], last[sub:]

    future = future.reshape(heads, HD, HD)

    grad_raw = jnp.einsum("the,she->hts", mixed_grad, value_heads, preferred_element_type=F32)
    grad_scores = jnp.where(allowed, grad_raw, F32(0.0)).astype(BF)
    query_grad = jnp.einsum(
        "hts,shd->thd", grad_scores, key_heads, preferred_element_type=F32
    ) + jnp.where(
        in_first,
        jnp.einsum("the,hde->thd", mixed_grad, prior, preferred_element_type=F32),
        F32(0.0),
    )
    key_grad = jnp.einsum(
        "hts,thd->shd", grad_scores, query_heads, preferred_element_type=F32
    ) + jnp.where(
        in_last,
        jnp.einsum("she,hde->shd", value_heads, future, preferred_element_type=F32),
        F32(0.0),
    )
    value_grad = jnp.einsum(
        "hts,the->she", weights, mixed_grad, preferred_element_type=F32
    ) + jnp.where(
        in_last,
        jnp.einsum("shd,hde->she", key_heads, future, preferred_element_type=F32),
        F32(0.0),
    )
    return (
        layer_out,
        query_grad.astype(BF).reshape(tok, width),
        key_grad.astype(BF).reshape(tok, width),
        value_grad.astype(BF).reshape(tok, width),
        weight_grad,
    )


def solution(mesh):
    grid = Mesh(mesh.devices.reshape(4, 8, 4, 2), ("y", "z", "x", "c"))
    return jax.shard_map(
        shards,
        mesh=grid,
        in_specs=(
            P(CTX, HEAD),
            P(CTX, HEAD),
            P(CTX, HEAD),
            P(CTX),
            P(CTX + HEAD, None),
            P(HEAD, CTX),
        ),
        out_specs=(
            P(CTX + HEAD, None),
            P(CTX, HEAD),
            P(CTX, HEAD),
            P(CTX, HEAD),
            P(HEAD + CTX, None),
        ),
        check_vma=False,
    )
```
